32 devices in a mesh: tx: 2 (over x), rx: 4 (over z), freq: 4 (over y, core).
Axes of the slice: x: 2, y: 2, z: 4, core: 2. Of those that a mesh axis runs over, the one named last changes fastest.
Arguments:
- spectrum: float32 [2, 8, 2048, 2048], P(None, 'freq', 'tx', 'rx'), may hold values from -6 to 6
- measured: float32 [2, 8, 2048, 2048], P(None, 'freq', 'tx', 'rx'), may hold values from -12 to 12
- wavenumber: float32 [8], replicated, may hold values from 1.5 to 3
- send_weight: float32 [2048], P('tx'), may hold values from 0.25 to 2
- hear_weight: float32 [2048], P('rx'), may hold values from 0.25 to 2
- aperture: int32 [128, 128], P('tx', 'rx'), may hold values 0 or 1
Outputs:
- updated: float32 [2, 8, 2048, 2048], P(None, 'freq', 'tx', 'rx')
- residual: float32 [2, 8, 2048, 2048], P(None, 'freq', 'tx', 'rx')
The draws below stay inside these ranges and needn't reach their ends.
Inputs may be any that keep to these rules, and one draw needn't show every extreme that they name: `aperture`: 1 marks a live tile of 16 x 16 antenna pairs, 0 a silent one.
All inputs are finite; a program needn't handle non-finite values. No bound on the sum of `aperture` on one device may be relied on, other than what follows from the above.
Results may differ from the reference program's by a relative error of at most 0.00016.
Values sent between devices are 32-bit elements; how exact they have to be, the bound alone decides.
A program may use at most 192 MiB of HBM per device.

```python
import math
import jax
import jax.numpy as jnp
from jax import lax

F = 8
NT = 2048
NR = 2048
TILE = 16
DEPTH = 8


def with_ends(values, rng, least, top_value):
    shape = values.shape
    spot = [jax.random.randint(jax.random.fold_in(rng, axis), (), 0, shape[axis]) for axis in range(len(shape))]
    values = values.at[tuple(spot)].set(least)
    longest = shape.index(max(shape))
    spot[longest] = (spot[longest] + 1) % shape[longest]
    return values.at[tuple(spot)].set(top_value)


def level_of(stream_key, extent, split, smallest, largest):
    factor_of, own = 1.0, jax.random.fold_in(stream_key, 6)
    for position, blocks in split:
        steps = jnp.exp(jax.random.uniform(jax.random.fold_in(own, position), (blocks,), jnp.float32, smallest / len(split), largest / len(split)))
        factor_of = factor_of * jnp.repeat(steps, extent[position] // blocks).reshape([-1 if axis == position else 1 for axis in range(len(extent))])
    return factor_of


def noise(key, shape, deviation, reach, pieces=(), kind=jnp.bfloat16):
    values = deviation * jax.random.normal(key, shape, jnp.float32)
    if pieces:
        values = values * level_of(key, shape, pieces, -0.22, 0.18)
    return jnp.clip(values, -reach, reach).astype(kind)


def setup_inputs(seed: int = 0) -> dict:
    streams_of = jax.random.split(jax.random.key(seed), 7)
    spectrum = noise(streams_of[0], (2, DEPTH, NT, NR), 1.0, 6.0, ((1, 4), (2, 2), (3, 4)), jnp.float32)
    measured = noise(streams_of[1], (2, F, NT, NR), 2.0, 12.0, ((1, 4), (2, 2), (3, 4)), jnp.float32)
    wavenumber = jnp.clip(jax.random.uniform(streams_of[2], (F,), jnp.float32, 1.5, 3.0), 1.5, 3.0)
    send_weight = jnp.clip(jnp.exp(math.log(2.0) - 2.0794415 * jax.random.uniform(streams_of[3], (NT,), jnp.float32) ** level_of(streams_of[3], (NT,), ((0, 2),), -0.2, 0.2)), 0.25, 2.0)
    hear_weight = jnp.clip(jnp.exp(math.log(2.0) - 2.0794415 * jax.random.uniform(streams_of[4], (NR,), jnp.float32) ** level_of(streams_of[4], (NR,), ((0, 4),), -0.2, 0.2)), 0.25, 2.0)
    aperture = with_ends((jax.random.randint(streams_of[5], (NT // TILE, NR // TILE), 0, 3) < 2).astype(jnp.int32), jax.random.fold_in(streams_of[5], 1), 0, 1)
    return dict(spectrum=spectrum, measured=measured, wavenumber=wavenumber, send_weight=send_weight, hear_weight=hear_weight, aperture=aperture)


depth_step = 2.0
step_size = 0.125
root_floor = 0.25

def wave_numbers(offset, length, total):
    indices = offset + jnp.arange(length, dtype=jnp.int32)
    signed = jnp.where(indices < total // 2, indices, indices - total)
    return 2.0 * jnp.pi / total * signed.astype(jnp.float32)

def vertical(wavenumber, waves_sent, waves_heard):
    squared = (wavenumber * wavenumber)[:, None, None]
    first_root = jnp.sqrt(jnp.maximum(squared - (waves_sent * waves_sent)[None, :, None], 0.0) + root_floor)
    second_root = jnp.sqrt(jnp.maximum(squared - (waves_heard * waves_heard)[None, None, :], 0.0) + root_floor)
    return first_root + second_root

def reference(spectrum, measured, wavenumber, send_weight, hear_weight, aperture):
    waves_sent = wave_numbers(0, NT, NT)
    waves_heard = wave_numbers(0, NR, NR)
    vertical_waves = vertical(wavenumber, waves_sent, waves_heard)
    pair_real = jnp.zeros((F, NT, NR), jnp.float32)
    pair_imag = jnp.zeros((F, NT, NR), jnp.float32)
    for depth_index in range(DEPTH):
        phases = vertical_waves * (depth_step * (depth_index + 1))
        cosine = jnp.cos(phases)
        sine_part = jnp.sin(phases)
        layer_real = spectrum[0, depth_index][None]
        layer_imag = spectrum[1, depth_index][None]
        pair_real = pair_real + (cosine * layer_real + sine_part * layer_imag)
        pair_imag = pair_imag + (cosine * layer_imag - sine_part * layer_real)
    field = jnp.fft.ifft2(lax.complex(pair_real, pair_imag), norm='ortho')
    tile_gate = jnp.repeat(jnp.repeat(aperture, TILE, axis=0), TILE, axis=1).astype(jnp.float32)
    weights = send_weight[:, None] * hear_weight[None, :] * tile_gate
    resid_real = weights[None] * (measured[0] - jnp.real(field))
    resid_imag = weights[None] * (measured[1] - jnp.imag(field))
    back = jnp.fft.fft2(lax.complex(resid_real, resid_imag), norm='ortho')
    back_real = jnp.real(back)
    back_imag = jnp.imag(back)
    layers_real = []
    layers_imag = []
    for depth_index in range(DEPTH):
        phases = vertical_waves * (depth_step * (depth_index + 1))
        cosine = jnp.cos(phases)
        sine_part = jnp.sin(phases)
        layers_real.append(lax.optimization_barrier(jnp.sum(cosine * back_real - sine_part * back_imag, axis=0)))
        layers_imag.append(lax.optimization_barrier(jnp.sum(cosine * back_imag + sine_part * back_real, axis=0)))
    gradient = jnp.stack([jnp.stack(layers_real), jnp.stack(layers_imag)])
    return (spectrum + step_size * gradient, jnp.stack([resid_real, resid_imag]))
```

```python
import math

import jax
import jax.numpy as jnp
from jax import lax
from jax.experimental import pallas as pl
from jax.sharding import PartitionSpec as P

depth_step = 2.0
step_size = 0.125
root_floor = 0.25
radix = 4


def roots(wavenumber, offset, length, total):
    indices = offset + jnp.arange(length, dtype=jnp.int32)
    signed = jnp.where(indices < total // 2, indices, indices - total)
    waves = 2.0 * jnp.pi / total * signed.astype(jnp.float32)
    squared = (wavenumber * wavenumber)[:, None] - (waves * waves)[None, :]
    return jnp.sqrt(jnp.maximum(squared, 0.0) + root_floor)


def unit_pair(outer, inner, period):
    product = (
        jnp.arange(outer, dtype=jnp.int32)[:, None] * jnp.arange(inner, dtype=jnp.int32)[None, :] % period
    )
    phases = 2.0 * math.pi / period * product.astype(jnp.float32)
    return jnp.cos(phases), jnp.sin(phases)


def dft_tables(total):
    width = total // radix
    base_cos, base_sin = unit_pair(width, width, width)
    turn_cos, turn_sin = unit_pair(radix, width, total)
    scale = 1.0 / math.sqrt(total)
    turn_cos = turn_cos[:, None, :] * scale
    turn_sin = turn_sin[:, None, :] * scale
    return (
        turn_cos * base_cos - turn_sin * base_sin,
        turn_cos * base_sin + turn_sin * base_cos,
    )


def dft(pieces, tables, form, sign):
    (ar, ai), (br, bi), (cr, ci), (dr, di) = [(x[0], x[1]) for x in pieces]
    er, ei, gr, gi = ar + cr, ai + ci, ar - cr, ai - ci
    hr, hi, kr, ki = br + dr, bi + di, sign * (br - dr), sign * (bi - di)
    mixed_real = jnp.stack([er + hr, gr - ki, er - hr, gr + ki])
    mixed_imag = jnp.stack([ei + hi, gi + kr, ei - hi, gi - kr])
    mixed = jnp.stack([mixed_real, mixed_imag], axis=1)
    cosine, sine = tables
    first = jnp.einsum(form, cosine, mixed, precision=lax.Precision.HIGH)
    second = jnp.einsum(form, sine, mixed, precision=lax.Precision.HIGH)
    return jnp.stack(
        [
            first[:, :, 0] - sign * second[:, :, 1],
            first[:, :, 1] + sign * second[:, :, 0],
        ]
    )


def unmix(done, blocks):
    total = done.shape[1] * done.shape[2]
    rows = total // math.prod(blocks)
    freqs, width = done.shape[3:]
    done = jnp.transpose(done, (2, 1, 0, 3, 4)).reshape((math.prod(blocks), rows, 2, freqs, width))
    return jnp.transpose(done, (0, 2, 3, 1, 4)).reshape(tuple(blocks) + (2, freqs, rows, width))


def quarters(chunks, axis):
    count = chunks.shape[0]
    if count >= radix and count % radix == 0:
        step = count // radix
        return [
            jnp.concatenate([chunks[q * step + k] for k in range(step)], axis=axis) for q in range(radix)
        ]
    whole = jnp.concatenate([chunks[k] for k in range(count)], axis=axis)
    return jnp.split(whole, radix, axis=axis)


def exchange(values, axes):
    return lax.all_to_all(values, axes, split_axis=0, concat_axis=0, tiled=True)


def pair_kernel(layers, sent, heard, out):
    depth, rows = layers.shape[1:3]
    for f in range(out.shape[1]):
        hr = heard[0, f : f + 1, :]
        hi = heard[1, f : f + 1, :]
        for start in range(0, rows, 8):
            block = slice(start, start + 8)
            sr = sent[0, block, f : f + 1]
            si = sent[1, block, f : f + 1]
            zr = sr * hr - si * hi
            zi = -(sr * hi + si * hr)
            ar = layers[0, depth - 1, block, :]
            ai = layers[1, depth - 1, block, :]
            for j in range(depth - 1, -1, -1):
                ar, ai = ar * zr - ai * zi, ar * zi + ai * zr
                if j:
                    ar = ar + layers[0, j - 1, block, :]
                    ai = ai + layers[1, j - 1, block, :]
            out[0, f, block, :] = ar
            out[1, f, block, :] = ai


def gradient_kernel(pieces, sent, heard, out):
    freqs, rows = pieces.shape[1:3]
    depth = out.shape[1]
    for start in range(0, rows, 8):
        block = slice(start, start + 8)
        sums = [None] * depth
        for f in range(freqs):
            hr = heard[0, f : f + 1, :]
            hi = heard[1, f : f + 1, :]
            sr = sent[0, block, f : f + 1]
            si = sent[1, block, f : f + 1]
            zr = sr * hr - si * hi
            zi = sr * hi + si * hr
            tr = step_size * pieces[0, f, block, :]
            ti = step_size * pieces[1, f, block, :]
            for j in range(depth):
                tr, ti = tr * zr - ti * zi, tr * zi + ti * zr
                if f:
                    sums[j] = (sums[j][0] + tr, sums[j][1] + ti)
                else:
                    sums[j] = (tr, ti)
        for j in range(depth):
            out[0, j, block, :] = sums[j][0]
            out[1, j, block, :] = sums[j][1]


def pointwise(kernel, values, sent, heard, planes):
    _, count, rows, width = values.shape
    freqs = heard.shape[1]
    height = min(rows, 32)
    lanes = min(width, 128)
    return pl.pallas_call(
        kernel,
        grid=(rows // height, width // lanes),
        in_specs=[
            pl.BlockSpec((2, count, height, lanes), lambda i, k: (0, 0, i, k)),
            pl.BlockSpec((2, height, freqs), lambda i, k: (0, i, 0)),
            pl.BlockSpec((2, freqs, lanes), lambda i, k: (0, 0, k)),
        ],
        out_specs=pl.BlockSpec((2, planes, height, lanes), lambda i, k: (0, 0, i, k)),
        out_shape=jax.ShapeDtypeStruct((2, planes, rows, width), jnp.float32),
    )(values, sent, heard)


def per_device(spectrum, measured, wavenumber, send_weight, hear_weight, aperture):
    _, depth_local, rows_sent, rows_heard = spectrum.shape
    freq_local = measured.shape[1]
    freq_total = wavenumber.shape[0]
    senders = lax.axis_size("tx")
    hearers = lax.axis_size("rx")
    layers = lax.axis_size("freq")
    depth = depth_local * layers
    total_sent = rows_sent * senders
    total_heard = rows_heard * hearers
    slab = rows_sent // layers
    strip = rows_heard // senders
    band = rows_sent // hearers

    first_row = lax.axis_index("tx") * rows_sent + lax.axis_index("freq") * slab
    sent_phase = depth_step * roots(wavenumber, first_row, slab, total_sent).T
    heard_phase = depth_step * roots(wavenumber, lax.axis_index("rx") * rows_heard, rows_heard, total_heard)
    sent = jnp.stack([jnp.cos(sent_phase), jnp.sin(sent_phase)])
    heard = jnp.stack([jnp.cos(heard_phase), jnp.sin(heard_phase)])
    tables_sent = dft_tables(total_sent)
    tables_heard = tables_sent if total_heard == total_sent else dft_tables(total_heard)
    near = "qsm,qcfmw->qscfw"
    far = "qsm,qcfwm->qscfw"

    split = spectrum.reshape(2, depth_local, layers, slab, rows_heard)
    split = exchange(jnp.transpose(split, (2, 0, 1, 3, 4)), "freq")
    stacked = jnp.transpose(split, (1, 0, 2, 3, 4)).reshape(2, depth, slab, rows_heard)
    pair = pointwise(pair_kernel, stacked, sent, heard, freq_total)

    pair = pair.reshape(2, layers, freq_local, slab, senders, strip)
    pair = jnp.transpose(pair, (4, 1, 0, 2, 3, 5)).reshape(senders * layers, 2, freq_local, slab, strip)
    pair = exchange(pair, ("tx", "freq"))
    done = dft(quarters(pair, 2), tables_sent, near, 1.0)
    done = exchange(unmix(done, (senders * hearers,)), ("tx", "rx"))
    done = done.reshape((senders, hearers) + done.shape[1:])
    done = jnp.swapaxes(done, 0, 1).reshape((senders * hearers,) + done.shape[2:])
    done = dft(quarters(done, 3), tables_heard, far, 1.0)
    done = exchange(unmix(done, (hearers,)), "rx")
    field = jnp.transpose(done, (1, 2, 0, 4, 3)).reshape(2, freq_local, rows_sent, rows_heard)

    tiles_sent, tiles_heard = aperture.shape
    gate = aperture.astype(jnp.float32)
    weights = (
        send_weight.reshape(tiles_sent, -1)[:, :, None, None]
        * gate[:, None, :, None]
        * hear_weight.reshape(tiles_heard, -1)[None, None, :, :]
    ).reshape(rows_sent, rows_heard)
    residual = weights[None, None] * (measured - field)

    back = residual.reshape(2, freq_local, hearers, band, rows_heard)
    back = exchange(jnp.transpose(back, (2, 0, 1, 3, 4)), "rx")
    done = dft(quarters(back, 3), tables_heard, far, -1.0)
    done = unmix(done, (hearers, senders))
    done = jnp.swapaxes(done, 0, 1).reshape((senders * hearers,) + done.shape[2:])
    done = exchange(done, ("tx", "rx"))
    done = dft(quarters(done, 3), tables_sent, far, -1.0)
    done = exchange(unmix(done, (senders * layers,)), ("tx", "freq"))
    done = done.reshape(senders, layers, 2, freq_local, slab, strip)
    pieces = jnp.transpose(done, (2, 1, 3, 4, 0, 5)).reshape(2, freq_total, slab, rows_heard)

    gradient = pointwise(gradient_kernel, pieces, sent, heard, depth)
    gradient = gradient.reshape(2, layers, depth_local, slab, rows_heard)
    gradient = exchange(jnp.transpose(gradient, (1, 0, 2, 3, 4)), "freq")
    gradient = jnp.transpose(gradient, (1, 2, 0, 3, 4)).reshape(spectrum.shape)
    return (spectrum + gradient, residual)


def solution(mesh):
    placed = (
        P(None, "freq", "tx", "rx"),
        P(None, "freq", "tx", "rx"),
        P(),
        P("tx"),
        P("rx"),
        P("tx", "rx"),
    )
    return jax.shard_map(
        per_device,
        mesh=mesh,
        in_specs=placed,
        out_specs=(P(None, "freq", "tx", "rx"), P(None, "freq", "tx", "rx")),
        check_vma=False,
    )
```
